512 devices in a mesh: en: 32 (over z, x_hi), ph: 4 (over y), blk: 4 (over x_lo, core).
Axes of the slice: x: 4 (x_hi: 2, x_lo: 2; x = x_hi * 2 + x_lo), y: 4, z: 16, core: 2. Of those that a mesh axis runs over, the one named last changes fastest.
Arguments:
- lesser_in: bfloat16 [96, 8, 512, 512], P('en', 'blk', 'ph'), may hold values from -6 to 6
- greater_in: bfloat16 [96, 8, 512, 512], P('en', 'blk', 'ph'), may hold values from -6 to 6
- inverse: bfloat16 [96, 8, 512, 512], P('en', 'blk', 'ph'), may hold values from -0.25 to 0.25
- offsets: int32 [96, 8], P('en', 'ph'), may hold values from -9 to 9, as said below
- couplings: float32 [96, 8], P('en', 'ph'), may hold values from 0.2 to 1
Outputs:
- lesser_out: bfloat16 [96, 8, 512, 512], P('en', 'blk', 'ph')
- greater_out: bfloat16 [96, 8, 512, 512], P('en', 'blk', 'ph')
The draws below stay inside these ranges and needn't reach their ends.
Inputs may be any that keep to these rules, and one draw needn't show every extreme that they name: `offsets`: both extremes occur in every draw.
All inputs are finite; a program needn't handle non-finite values.
Results may differ from the reference program's by a relative error of at most 0.0057.
Values may be sent and summed in bfloat16 or wider, within the bound.
A program may use at most 64 MiB of HBM per device.

```python
import math
import jax
import jax.numpy as jnp
from jax import lax

O = 512
MAXOFF = 9
NE = 96
NB = 8
K = 8


def draw_offsets(key, part):
    values = jax.random.randint(key, (NE, K), -MAXOFF, MAXOFF + 1, dtype=jnp.int32)
    values = values.at[0, 0].set(MAXOFF)
    values = values.at[NE - 1, 0].set(-MAXOFF)
    return values


def levels(key, extent, shards, smallest, top_value):
    level, own = 1.0, jax.random.fold_in(key, 6)
    for position, blocks in shards:
        steps = jnp.exp(jax.random.uniform(jax.random.fold_in(own, position), (blocks,), jnp.float32, smallest / len(shards), top_value / len(shards)))
        level = level * jnp.repeat(steps, extent[position] // blocks).reshape([-1 if axis == position else 1 for axis in range(len(extent))])
    return level


def centred(own_key, dims, spread, bound, shards=(), kind=jnp.bfloat16):
    result = jax.random.normal(own_key, dims, jnp.float32) * spread
    if len(shards) > 0:
        result = levels(own_key, dims, shards, -0.22, 0.18) * result
    return jnp.clip(result, min=-bound, max=bound).astype(kind)


def setup_inputs(seed: int = 0) -> dict:
    keys = jax.random.split(jax.random.key(seed), 6)
    return {
        "lesser_in": centred(keys[0], (NE, NB, O, O), 1.0, 6.0, ((0, 32), (1, 4), (2, 4))),
        "greater_in": centred(keys[1], (NE, NB, O, O), 1.0, 6.0, ((0, 32), (1, 4), (2, 4))),
        "inverse": centred(keys[2], (NE, NB, O, O), O ** -0.5, 0.25, ((0, 32), (1, 4), (2, 4))),
        "offsets": draw_offsets(jax.random.fold_in(keys[5], 71), 0),
        "couplings": jnp.clip(jnp.exp(math.log(1.0) - 1.609438 * jax.random.uniform(keys[4], (NE, K), jnp.float32) ** levels(keys[4], (NE, K), ((0, 32), (1, 4)), -0.2, 0.2)), 0.2, 1.0),
    }


def reference(lesser_in, greater_in, inverse, offsets, couplings):
    padding = jnp.zeros((MAXOFF,) + lesser_in.shape[1:], jnp.bfloat16)
    lesser_pad = jnp.concatenate([padding, lesser_in, padding], axis=0)
    greater_pad = jnp.concatenate([padding, greater_in, padding], axis=0)

    def per_energy(packed):
        energy, shifts, weights, inverse_n = packed
        source = (energy + shifts + MAXOFF).astype(jnp.int32)
        inverse_f32 = inverse_n.astype(jnp.float32)
        results = []
        for padded in (lesser_pad, greater_pad):
            shifted = jnp.take(padded, source, axis=0).astype(jnp.float32)
            self_energy = jnp.einsum("k,kbij->bij", weights.astype(jnp.float32), shifted, precision=lax.Precision.HIGHEST).astype(jnp.bfloat16)
            left_product = jnp.einsum("bik,bkj->bij", inverse_f32, self_energy.astype(jnp.float32), precision=lax.Precision.HIGHEST).astype(jnp.bfloat16)
            results.append(jnp.einsum("bik,bjk->bij", left_product.astype(jnp.float32), inverse_f32, precision=lax.Precision.HIGHEST).astype(jnp.bfloat16))
        return results[0], results[1]

    energies = jnp.arange(NE, dtype=jnp.int32)
    lesser_out, greater_out = lax.map(per_energy, (energies, offsets, couplings, inverse))
    return lesser_out, greater_out
```

```python
import functools

import jax
import jax.numpy as jnp
from jax import lax
from jax.experimental import pallas as pl
from jax.experimental.pallas import tpu as pltpu
from jax.sharding import PartitionSpec as P

MESH = pl.DeviceIdType.MESH
MAXOFF = 9
CHUNKS = 4
EXTRA = 3
ROWS = 64


def owner(chunk, j):
    if j == 2:
        return (chunk + 2) % 4
    return 2 * j + 1 - chunk % 2


def kernel(
    n_en, offs_ref, coup_ref, less_ref, great_ref, inv_ref,
    less_out, great_out,
    win0, win1, win2, win3, sig, whole, invs, prod, offs_v, coup_v, offs_s, coup_s,
    win_recv, x_send, z_send, sig_send, sig_recv, inv_send, inv_recv,
    out_send, out_recv, meta_send, meta_recv, smem_sem,
):
    wins = (win0, win1, win2, win3)
    en, y = lax.axis_index("en"), lax.axis_index("ph")
    h = lax.rem(en, 2)
    base = en - h
    up = {"en": lax.rem(en + 2, n_en)}
    down = {"en": lax.rem(en + n_en - 2, n_en)}
    partner = {"en": base + 1 - h}

    def group_member(d):
        return {"en": base + lax.rem(h + d // 4, 2), "ph": lax.rem(y + d % 4, 4)}

    barrier = pltpu.get_barrier_semaphore()
    pl.semaphore_signal(barrier, inc=1, device_id=up, device_id_type=MESH)
    pl.semaphore_signal(barrier, inc=1, device_id=down, device_id_type=MESH)
    for d in range(1, 8):
        pl.semaphore_signal(barrier, inc=1, device_id=group_member(d), device_id_type=MESH)
    pl.semaphore_wait(barrier, 9)

    def remote(src, dst, send, recv, device):
        return pltpu.make_async_remote_copy(
            src_ref=src, dst_ref=dst, send_sem=send, recv_sem=recv, device_id=device, device_id_type=MESH
        )

    def source(chunk, half):
        ref = (less_ref, great_ref)[chunk // 2]
        return ref.at[:, chunk % 2, pl.ds(pl.multiple_of(half * ROWS, ROWS), ROWS), :]

    def group(chunk, g):
        return wins[chunk].at[pl.ds(3 * g, 3)]

    def wait_group(chunk, g):
        pltpu.make_async_copy(group(chunk, g), group(chunk, g), win_recv.at[chunk, g]).wait()

    def own_local(chunk):
        return pltpu.make_async_copy(source(chunk, h), group(chunk, 3 + h), win_recv.at[chunk, 3 + h])

    def exchange(chunk):
        return remote(source(chunk, 1 - h), group(chunk, 3 + h), x_send.at[chunk], win_recv.at[chunk, 3 + h], partner)

    def own(chunk):
        src = source(chunk, h)
        return (
            remote(src, group(chunk, 1 + h), z_send.at[chunk, 0], win_recv.at[chunk, 1 + h], up),
            remote(src, group(chunk, 5 + h), z_send.at[chunk, 1], win_recv.at[chunk, 5 + h], down),
        )

    def passed(chunk):
        src = group(chunk, 4 - h)
        return (
            remote(src, group(chunk, 2 - h), z_send.at[chunk, 2], win_recv.at[chunk, 2 - h], up),
            remote(src, group(chunk, 6 - h), z_send.at[chunk, 3], win_recv.at[chunk, 6 - h], down),
        )

    def relay(chunk):
        return (
            remote(group(chunk, 2), group(chunk, 0), z_send.at[chunk, 4], win_recv.at[chunk, 0], up),
            remote(group(chunk, 5), group(chunk, 7), z_send.at[chunk, 5], win_recv.at[chunk, 7], down),
        )

    def start(copies):
        for copy in copies:
            copy.start()

    def inv_part(slot, to):
        if slot == 0:
            return inv_ref.at[to // 2, 1 - lax.rem(to, 2)]
        return inv_ref.at[2, lax.rem(to, 2)]

    def inv_copy(slot, d):
        to = lax.rem(y + d, 4)
        return remote(inv_part(slot, to), invs.at[slot, y], inv_send.at[slot, d - 1], inv_recv.at[slot, y], {"ph": to})

    def meta_copies(d):
        me = 4 * h + y
        to = group_member(d)
        return (
            remote(offs_ref, offs_v.at[me], meta_send.at[0, d], meta_recv.at[0, me], to),
            remote(coup_ref, coup_v.at[me], meta_send.at[1, d], meta_recv.at[1, me], to),
        )

    exchange(0).start()
    start(own(0))
    me = 4 * h + y
    pltpu.make_async_copy(offs_ref, offs_v.at[me], meta_recv.at[0, me]).start()
    pltpu.make_async_copy(coup_ref, coup_v.at[me], meta_recv.at[1, me]).start()
    for d in range(1, 8):
        start(meta_copies(d))
    start(own(1))
    for chunk in range(1, CHUNKS):
        exchange(chunk).start()
    for slot in range(2):
        pltpu.make_async_copy(inv_part(slot, y), invs.at[slot, y], inv_recv.at[slot, y]).start()
        for d in range(1, 4):
            inv_copy(slot, d).start()
    for chunk in range(CHUNKS):
        own_local(chunk).start()

    def forward(chunk):
        wait_group(chunk, 4 - h)
        start(passed(chunk))

    def relays(chunk):
        wait_group(chunk, 2)
        wait_group(chunk, 5)
        start(relay(chunk))

    def gather_meta():
        for m in range(8):
            pltpu.make_async_copy(offs_v.at[m], offs_v.at[m], meta_recv.at[0, m]).wait()
            pltpu.make_async_copy(coup_v.at[m], coup_v.at[m], meta_recv.at[1, m]).wait()
        first = pltpu.make_async_copy(offs_v, offs_s, smem_sem.at[0])
        second = pltpu.make_async_copy(coup_v, coup_s, smem_sem.at[1])
        first.start()
        second.start()
        first.wait()
        second.wait()

    def sigma_copy(chunk, n):
        to = {"en": base + n // 3, "ph": owner(chunk, n % 3)}
        part = 2 * y + h
        return remote(
            sig.at[chunk, n], whole.at[chunk, part], sig_send.at[chunk, n], sig_recv.at[chunk, part], to
        )

    def is_own(chunk, n):
        return jnp.logical_and(h == n // 3, y == owner(chunk, n % 3))

    def mix(chunk):
        for g in (0, 1, 6, 7):
            wait_group(chunk, g)
        wait_group(chunk, 3 + h)
        window = wins[chunk]

        def body(step, _):
            i = step // 2
            rows = pl.ds(pl.multiple_of(32 * lax.rem(step, 2), 32), 32)
            total = jnp.zeros((32, window.shape[2]), jnp.float32)
            for k in range(8):
                m = 4 * (i // 3) + k // 2
                offset = offs_s[m, lax.rem(i, 3), k % 2]
                energy = 3 * base + i + offset
                inside = jnp.logical_and(energy >= 0, energy < 3 * n_en)
                weight = jnp.where(inside, coup_s[m, lax.rem(i, 3), k % 2], jnp.float32(0.0))
                total = total + weight * window[i + offset + MAXOFF, rows, :].astype(jnp.float32)
            sig[chunk, i, rows, :] = total.astype(jnp.bfloat16)
            return 0

        lax.fori_loop(0, 12, body, 0)
        part = 2 * y + h
        for n in range(6):
            mine = is_own(chunk, n)

            @pl.when(mine)
            def _():
                pltpu.make_async_copy(sig.at[chunk, n], whole.at[chunk, part], sig_recv.at[chunk, part]).start()

            @pl.when(jnp.logical_not(mine))
            def _():
                sigma_copy(chunk, n).start()

    def out_ref(chunk, j):
        return (less_out, great_out)[chunk // 2].at[j, chunk % 2]

    def energy_of(chunk):
        return jnp.where(y == (chunk + 2) % 4, 2, y // 2)

    def out_copy(chunk, d):
        to = lax.rem(y + d, 4)
        j = energy_of(chunk)
        return remote(prod.at[chunk, to], out_ref(chunk, j), out_send.at[chunk, d], out_recv.at[chunk, j], {"ph": to})

    def multiply(chunk):
        @pl.when(y != chunk)
        def _():
            slot = jnp.where(y == (chunk + 2) % 4, 1, 0)
            for part in range(8):
                pltpu.make_async_copy(
                    whole.at[chunk, part], whole.at[chunk, part], sig_recv.at[chunk, part]
                ).wait()
            sigma = whole[chunk].reshape(512, 512)
            inverse = invs[slot].reshape(512, 512)

            for r in range(2):
                rows = invs[slot, pl.ds(2 * r, 2)].reshape(256, 512)
                left = jnp.dot(rows, sigma, preferred_element_type=jnp.float32).astype(jnp.bfloat16)
                result = lax.dot_general(
                    left, inverse, (((1,), (1,)), ((), ())), preferred_element_type=jnp.float32
                )
                prod[chunk, pl.ds(2 * r, 2)] = result.astype(jnp.bfloat16).reshape(2, 128, 512)
            for d in (2, 1, 3):
                out_copy(chunk, d).start()
            j = energy_of(chunk)
            pltpu.make_async_copy(prod.at[chunk, y], out_ref(chunk, j), out_recv.at[chunk, j]).start()

    forward(0)
    start(own(2))
    gather_meta()
    relays(0)
    forward(1)
    start(own(3))
    mix(0)
    relays(1)
    forward(2)
    for slot in range(2):
        for part in range(4):
            pltpu.make_async_copy(invs.at[slot, part], invs.at[slot, part], inv_recv.at[slot, part]).wait()
    multiply(0)
    mix(1)
    relays(2)
    forward(3)
    multiply(1)
    mix(2)
    relays(3)
    multiply(2)
    mix(3)
    multiply(3)

    for chunk in range(CHUNKS):
        exchange(chunk).wait_send()
        for copy in own(chunk) + passed(chunk) + relay(chunk):
            copy.wait_send()
        for n in range(6):

            @pl.when(jnp.logical_not(is_own(chunk, n)))
            def _():
                sigma_copy(chunk, n).wait_send()

        @pl.when(y != chunk)
        def _():
            for d in range(1, 4):
                out_copy(chunk, d).wait_send()

    for slot in range(2):
        for d in range(1, 4):
            inv_copy(slot, d).wait_send()
    for d in range(1, 8):
        for copy in meta_copies(d):
            copy.wait_send()
    for chunk in range(CHUNKS):
        for j in range(3):
            pltpu.make_async_copy(out_ref(chunk, j), out_ref(chunk, j), out_recv.at[chunk, j]).wait()


def on_device(n_en, lesser_in, greater_in, inverse, offsets, couplings):
    bf16 = jnp.bfloat16
    dma = pltpu.SemaphoreType.DMA
    any_space = pl.BlockSpec(memory_space=pl.ANY)
    vmem = pl.BlockSpec(memory_space=pltpu.VMEM)
    width = lesser_in.shape[-1]
    window = pltpu.VMEM((24, ROWS, width), bf16)
    return pl.pallas_call(
        functools.partial(kernel, n_en),
        out_shape=(
            jax.ShapeDtypeStruct(lesser_in.shape, bf16),
            jax.ShapeDtypeStruct(greater_in.shape, bf16),
        ),
        in_specs=[vmem, vmem, any_space, any_space, any_space],
        out_specs=(any_space, any_space),
        scratch_shapes=[
            window, window, window, window,
            pltpu.VMEM((CHUNKS, 6, ROWS, width), bf16),
            pltpu.VMEM((CHUNKS, 8, ROWS, width), bf16),
            pltpu.VMEM((2, 4, 128, width), bf16),
            pltpu.VMEM((CHUNKS, 4, 128, width), bf16),
            pltpu.VMEM((8, 3, 2), jnp.int32),
            pltpu.VMEM((8, 3, 2), jnp.float32),
            pltpu.SMEM((8, 3, 2), jnp.int32),
            pltpu.SMEM((8, 3, 2), jnp.float32),
            dma((CHUNKS, 8)),
            dma((CHUNKS,)),
            dma((CHUNKS, 6)),
            dma((CHUNKS, 6)),
            dma((CHUNKS, 8)),
            dma((2, 3)),
            dma((2, 4)),
            dma((CHUNKS, 4)),
            dma((CHUNKS, 3)),
            dma((2, 8)),
            dma((2, 8)),
            dma((2,)),
        ],
        compiler_params=pltpu.CompilerParams(collective_id=0, has_side_effects=True),
        name="born_update",
    )(offsets, couplings, lesser_in, greater_in, inverse)


def solution(mesh):
    blocks = P("en", "blk", "ph", None)
    placed = (blocks, blocks, blocks, P("en", "ph"), P("en", "ph"))
    return jax.shard_map(
        functools.partial(on_device, mesh.shape["en"]),
        mesh=mesh,
        in_specs=placed,
        out_specs=(blocks, blocks),
        check_vma=False,
    )
```

```python
import functools

import jax
import jax.numpy as jnp
from jax import lax
from jax.experimental import pallas as pl
from jax.experimental.pallas import tpu as pltpu
from jax.sharding import PartitionSpec as P

MESH = pl.DeviceIdType.MESH
MAXOFF = 9
CHUNKS = 4
EXTRA = 3
ROWS = 64


def owner(chunk, j):
    if j == 2:
        return (chunk + 2) % 4
    return 2 * j + 1 - chunk % 2


def kernel(
    n_en, offs_ref, coup_ref, less_ref, great_ref, inv_ref,
    less_out, great_out,
    win0, win1, win2, win3, sig, whole, invs, prod, offs_v, coup_v, offs_s, coup_s,
    win_recv, x_send, z_send, sig_send, sig_recv, inv_send, inv_recv,
    out_send, out_recv, meta_send, meta_recv, smem_sem,
):
    wins = (win0, win1, win2, win3)
    en, y = lax.axis_index("en"), lax.axis_index("ph")
    h = lax.rem(en, 2)
    base = en - h
    above, below = en + 2 < n_en, en >= 2
    two_above, two_below = en + 4 < n_en, en >= 4
    up = {"en": lax.rem(en + 2, n_en)}
    down = {"en": lax.rem(en + n_en - 2, n_en)}
    partner = {"en": base + 1 - h}

    def group_member(d):
        return {"en": base + lax.rem(h + d // 4, 2), "ph": lax.rem(y + d % 4, 4)}

    barrier = pltpu.get_barrier_semaphore()
    for side, there in ((up, above), (down, below)):

        @pl.when(there)
        def _():
            pl.semaphore_signal(barrier, inc=1, device_id=side, device_id_type=MESH)

    for d in range(1, 8):
        pl.semaphore_signal(barrier, inc=1, device_id=group_member(d), device_id_type=MESH)
    pl.semaphore_wait(barrier, 7 + above.astype(jnp.int32) + below.astype(jnp.int32))

    def remote(src, dst, send, recv, device):
        return pltpu.make_async_remote_copy(
            src_ref=src, dst_ref=dst, send_sem=send, recv_sem=recv, device_id=device, device_id_type=MESH
        )

    passes = (jnp.logical_and(above, below),) * 2

    def source(chunk, half):
        ref = (less_ref, great_ref)[chunk // 2]
        return ref.at[:, chunk % 2, pl.ds(pl.multiple_of(half * ROWS, ROWS), ROWS), :]

    def group(chunk, g):
        return wins[chunk].at[pl.ds(3 * g, 3)]

    def wait_group(chunk, g):
        pltpu.make_async_copy(group(chunk, g), group(chunk, g), win_recv.at[chunk, g]).wait()

    def own_local(chunk):
        return pltpu.make_async_copy(source(chunk, h), group(chunk, 3 + h), win_recv.at[chunk, 3 + h])

    def exchange(chunk):
        return remote(source(chunk, 1 - h), group(chunk, 3 + h), x_send.at[chunk], win_recv.at[chunk, 3 + h], partner)

    def own(chunk):
        src = source(chunk, h)
        return (
            remote(src, group(chunk, 1 + h), z_send.at[chunk, 0], win_recv.at[chunk, 1 + h], up),
            remote(src, group(chunk, 5 + h), z_send.at[chunk, 1], win_recv.at[chunk, 5 + h], down),
        )

    def passed(chunk):
        src = group(chunk, 4 - h)
        return (
            remote(src, group(chunk, 2 - h), z_send.at[chunk, 2], win_recv.at[chunk, 2 - h], up),
            remote(src, group(chunk, 6 - h), z_send.at[chunk, 3], win_recv.at[chunk, 6 - h], down),
        )

    def planes(chunk):
        return (
            remote(group(chunk, 4), group(chunk, 2), z_send.at[chunk, 0], win_recv.at[chunk, 2], up),
            remote(group(chunk, 3), group(chunk, 5), z_send.at[chunk, 1], win_recv.at[chunk, 5], down),
            remote(group(chunk, 3), group(chunk, 1), z_send.at[chunk, 2], win_recv.at[chunk, 1], up),
            remote(group(chunk, 4), group(chunk, 6), z_send.at[chunk, 3], win_recv.at[chunk, 6], down),
        )

    def relay(chunk):
        return (
            remote(group(chunk, 2), group(chunk, 0), z_send.at[chunk, 4], win_recv.at[chunk, 0], up),
            remote(group(chunk, 5), group(chunk, 7), z_send.at[chunk, 5], win_recv.at[chunk, 7], down),
        )

    def each(copies, act, conditions):
        for copy, there in zip(copies, conditions):

            @pl.when(there)
            def _():
                act(copy)

    def start(copies, conditions=None):
        each(copies, lambda copy: copy.start(), conditions or (above, below))

    def wait_groups(chunk, groups):
        there = (two_below, below, below, True, True, above, above, two_above)
        for g in groups:
            if there[g] is True:
                wait_group(chunk, g)
            else:
                pl.when(there[g])(functools.partial(wait_group, chunk, g))

    def inv_part(slot, to):
        if slot == 0:
            return inv_ref.at[to // 2, 1 - lax.rem(to, 2)]
        return inv_ref.at[2, lax.rem(to, 2)]

    def inv_copy(slot, d):
        to = lax.rem(y + d, 4)
        return remote(inv_part(slot, to), invs.at[slot, y], inv_send.at[slot, d - 1], inv_recv.at[slot, y], {"ph": to})

    def meta_copies(d):
        me = 4 * h + y
        to = group_member(d)
        return (
            remote(offs_ref, offs_v.at[me], meta_send.at[0, d], meta_recv.at[0, me], to),
            remote(coup_ref, coup_v.at[me], meta_send.at[1, d], meta_recv.at[1, me], to),
        )

    exchange(0).start()
    start(own(0))
    me = 4 * h + y
    pltpu.make_async_copy(offs_ref, offs_v.at[me], meta_recv.at[0, me]).start()
    pltpu.make_async_copy(coup_ref, coup_v.at[me], meta_recv.at[1, me]).start()
    for d in range(1, 8):
        for copy in meta_copies(d):
            copy.start()
    start(own(1))
    for chunk in range(1, CHUNKS):
        exchange(chunk).start()
    for slot in range(2):
        pltpu.make_async_copy(inv_part(slot, y), invs.at[slot, y], inv_recv.at[slot, y]).start()
        for d in range(1, 4):
            inv_copy(slot, d).start()
    for chunk in range(CHUNKS):
        own_local(chunk).start()

    def forward(chunk):
        if chunk < 2:
            wait_group(chunk, 4 - h)
            start(passed(chunk))
        else:
            wait_group(chunk, 3)
            wait_group(chunk, 4)
            start(planes(chunk), (above, below, above, below))

    def relays(chunk):
        wait_groups(chunk, (2, 5))
        start(relay(chunk), passes)

    def gather_meta():
        for m in range(8):
            pltpu.make_async_copy(offs_v.at[m], offs_v.at[m], meta_recv.at[0, m]).wait()
            pltpu.make_async_copy(coup_v.at[m], coup_v.at[m], meta_recv.at[1, m]).wait()
        first = pltpu.make_async_copy(offs_v, offs_s, smem_sem.at[0])
        second = pltpu.make_async_copy(coup_v, coup_s, smem_sem.at[1])
        first.start()
        second.start()
        first.wait()
        second.wait()

    def sigma_copy(chunk, n):
        to = {"en": base + n // 3, "ph": owner(chunk, n % 3)}
        part = 2 * y + h
        return remote(
            sig.at[chunk, n], whole.at[chunk, part], sig_send.at[chunk, n], sig_recv.at[chunk, part], to
        )

    def is_own(chunk, n):
        return jnp.logical_and(h == n // 3, y == owner(chunk, n % 3))

    def mix(chunk):
        wait_groups(chunk, (1, 6, 0, 7))
        if chunk < 2:
            wait_group(chunk, 3 + h)
        window = wins[chunk]

        def body(step, _):
            i = step // 2
            rows = pl.ds(pl.multiple_of(32 * lax.rem(step, 2), 32), 32)
            total = jnp.zeros((32, window.shape[2]), jnp.float32)
            for k in range(8):
                m = 4 * (i // 3) + k // 2
                offset = offs_s[m, k % 2, lax.rem(i, 3)]
                energy = 3 * base + i + offset
                inside = jnp.logical_and(energy >= 0, energy < 3 * n_en)
                weight = jnp.where(inside, coup_s[m, k % 2, lax.rem(i, 3)], jnp.float32(0.0))
                slot = jnp.where(inside, i + offset + MAXOFF, MAXOFF)
                total = total + weight * window[slot, rows, :].astype(jnp.float32)
            sig[chunk, i, rows, :] = total.astype(jnp.bfloat16)
            return 0

        lax.fori_loop(0, 12, body, 0)
        part = 2 * y + h
        for n in range(6):
            mine = is_own(chunk, n)

            @pl.when(mine)
            def _():
                pltpu.make_async_copy(sig.at[chunk, n], whole.at[chunk, part], sig_recv.at[chunk, part]).start()

            @pl.when(jnp.logical_not(mine))
            def _():
                sigma_copy(chunk, n).start()

    def out_ref(chunk, j):
        return (less_out, great_out)[chunk // 2].at[j, chunk % 2]

    def energy_of(chunk):
        return jnp.where(y == (chunk + 2) % 4, 2, y // 2)

    def out_copy(chunk, d):
        to = lax.rem(y + d, 4)
        j = energy_of(chunk)
        return remote(prod.at[chunk, to], out_ref(chunk, j), out_send.at[chunk, d], out_recv.at[chunk, j], {"ph": to})

    def multiply(chunk):
        @pl.when(y != chunk)
        def _():
            slot = jnp.where(y == (chunk + 2) % 4, 1, 0)
            for part in range(8):
                pltpu.make_async_copy(
                    whole.at[chunk, part], whole.at[chunk, part], sig_recv.at[chunk, part]
                ).wait()
            sigma = whole[chunk].reshape(512, 512)
            inverse = invs[slot].reshape(512, 512)

            for r in range(2):
                rows = invs[slot, pl.ds(2 * r, 2)].reshape(256, 512)
                left = jnp.dot(rows, sigma, preferred_element_type=jnp.float32).astype(jnp.bfloat16)
                result = lax.dot_general(
                    left, inverse, (((1,), (1,)), ((), ())), preferred_element_type=jnp.float32
                )
                prod[chunk, pl.ds(2 * r, 2)] = result.astype(jnp.bfloat16).reshape(2, 128, 512)
            for d in (2, 1, 3):
                out_copy(chunk, d).start()
            j = energy_of(chunk)
            pltpu.make_async_copy(prod.at[chunk, y], out_ref(chunk, j), out_recv.at[chunk, j]).start()

    def gather_inverses():
        for slot in range(2):
            for part in range(4):
                pltpu.make_async_copy(invs.at[slot, part], invs.at[slot, part], inv_recv.at[slot, part]).wait()

    forward(0)
    gather_meta()
    forward(1)
    relays(0)
    relays(1)
    forward(2)
    mix(0)
    mix(1)
    relays(2)
    forward(3)
    gather_inverses()
    multiply(0)
    mix(2)
    multiply(1)
    relays(3)
    multiply(2)
    mix(3)
    multiply(3)

    for chunk in range(CHUNKS):
        exchange(chunk).wait_send()
        sent = (own(chunk) + passed(chunk) if chunk < 2 else planes(chunk)) + relay(chunk)
        each(sent, lambda copy: copy.wait_send(), (above, below, above, below) + passes)
        for n in range(6):

            @pl.when(jnp.logical_not(is_own(chunk, n)))
            def _():
                sigma_copy(chunk, n).wait_send()

        @pl.when(y != chunk)
        def _():
            for d in range(1, 4):
                out_copy(chunk, d).wait_send()

    for slot in range(2):
        for d in range(1, 4):
            inv_copy(slot, d).wait_send()
    for d in range(1, 8):
        for copy in meta_copies(d):
            copy.wait_send()
    for chunk in range(CHUNKS):
        for j in range(3):
            pltpu.make_async_copy(out_ref(chunk, j), out_ref(chunk, j), out_recv.at[chunk, j]).wait()


def on_device(n_en, lesser_in, greater_in, inverse, offsets, couplings):
    bf16 = jnp.bfloat16
    dma = pltpu.SemaphoreType.DMA
    any_space = pl.BlockSpec(memory_space=pl.ANY)
    vmem = pl.BlockSpec(memory_space=pltpu.VMEM)
    width = lesser_in.shape[-1]
    window = pltpu.VMEM((24, ROWS, width), bf16)
    return pl.pallas_call(
        functools.partial(kernel, n_en),
        out_shape=(
            jax.ShapeDtypeStruct(lesser_in.shape, bf16),
            jax.ShapeDtypeStruct(greater_in.shape, bf16),
        ),
        in_specs=[vmem, vmem, any_space, any_space, any_space],
        out_specs=(any_space, any_space),
        scratch_shapes=[
            window, window, window, window,
            pltpu.VMEM((CHUNKS, 6, ROWS, width), bf16),
            pltpu.VMEM((CHUNKS, 8, ROWS, width), bf16),
            pltpu.VMEM((2, 4, 128, width), bf16),
            pltpu.VMEM((CHUNKS, 4, 128, width), bf16),
            pltpu.VMEM((8, 2, 3), jnp.int32),
            pltpu.VMEM((8, 2, 3), jnp.float32),
            pltpu.SMEM((8, 2, 3), jnp.int32),
            pltpu.SMEM((8, 2, 3), jnp.float32),
            dma((CHUNKS, 8)),
            dma((CHUNKS,)),
            dma((CHUNKS, 6)),
            dma((CHUNKS, 6)),
            dma((CHUNKS, 8)),
            dma((2, 3)),
            dma((2, 4)),
            dma((CHUNKS, 4)),
            dma((CHUNKS, 3)),
            dma((2, 8)),
            dma((2, 8)),
            dma((2,)),
        ],
        compiler_params=pltpu.CompilerParams(collective_id=0, has_side_effects=True, vmem_limit_bytes=40 * 1024 * 1024),
        name="born_update",
    )(offsets.T, couplings.T, *(pltpu.with_memory_space_constraint(a, pltpu.HBM) for a in (lesser_in, greater_in, inverse)))


def solution(mesh):
    blocks = P("en", "blk", "ph", None)
    placed = (blocks, blocks, blocks, P("en", "ph"), P("en", "ph"))
    return jax.shard_map(
        functools.partial(on_device, mesh.shape["en"]),
        mesh=mesh,
        in_specs=placed,
        out_specs=(blocks, blocks),
        check_vma=False,
    )
```

```python
import functools

import jax
import jax.numpy as jnp
from jax import lax
from jax.experimental import pallas as pl
from jax.experimental.pallas import tpu as pltpu
from jax.sharding import PartitionSpec as P

MESH = pl.DeviceIdType.MESH
MAXOFF = 9
CHUNKS = 4
EXTRA = 3
ROWS = 64


def owner(chunk, j):
    if j == 2:
        return (chunk + 2) % 4
    return 2 * j + 1 - chunk % 2


def kernel(
    n_en, offs_ref, coup_ref, less_ref, great_ref, inv_ref,
    less_out, great_out,
    win0, win1, win2, win3, sig, whole, invs, prod, offs_v, coup_v, offs_s, coup_s,
    win_recv, x_send, z_send, sig_send, sig_recv, inv_send, inv_recv,
    out_send, out_recv, meta_send, meta_recv, smem_sem,
):
    wins = (win0, win1, win2, win3)
    en, y = lax.axis_index("en"), lax.axis_index("ph")
    h = lax.rem(en, 2)
    base = en - h
    above, below = en + 2 < n_en, en >= 2
    two_above, two_below = en + 4 < n_en, en >= 4
    up = {"en": lax.rem(en + 2, n_en)}
    down = {"en": lax.rem(en + n_en - 2, n_en)}
    partner = {"en": base + 1 - h}

    def group_member(d):
        return {"en": base + lax.rem(h + d // 4, 2), "ph": lax.rem(y + d % 4, 4)}

    barrier = pltpu.get_barrier_semaphore()
    for side, there in ((up, above), (down, below)):

        @pl.when(there)
        def _():
            pl.semaphore_signal(barrier, inc=1, device_id=side, device_id_type=MESH)

    for d in range(1, 8):
        pl.semaphore_signal(barrier, inc=1, device_id=group_member(d), device_id_type=MESH)
    pl.semaphore_wait(barrier, 7 + above.astype(jnp.int32) + below.astype(jnp.int32))

    def remote(src, dst, send, recv, device):
        return pltpu.make_async_remote_copy(
            src_ref=src, dst_ref=dst, send_sem=send, recv_sem=recv, device_id=device, device_id_type=MESH
        )

    passes = (jnp.logical_and(above, below),) * 2

    def source(chunk, half):
        ref = (less_ref, great_ref)[chunk // 2]
        return ref.at[:, chunk % 2, pl.ds(pl.multiple_of(half * ROWS, ROWS), ROWS), :]

    def group(chunk, g):
        return wins[chunk].at[pl.ds(3 * g, 3)]

    def wait_group(chunk, g):
        pltpu.make_async_copy(group(chunk, g), group(chunk, g), win_recv.at[chunk, g]).wait()

    def own_local(chunk):
        return pltpu.make_async_copy(source(chunk, h), group(chunk, 3 + h), win_recv.at[chunk, 3 + h])

    def exchange(chunk):
        return remote(source(chunk, 1 - h), group(chunk, 3 + h), x_send.at[chunk], win_recv.at[chunk, 3 + h], partner)

    def own(chunk):
        src = source(chunk, h)
        return (
            remote(src, group(chunk, 1 + h), z_send.at[chunk, 0], win_recv.at[chunk, 1 + h], up),
            remote(src, group(chunk, 5 + h), z_send.at[chunk, 1], win_recv.at[chunk, 5 + h], down),
        )

    def passed(chunk):
        src = group(chunk, 4 - h)
        return (
            remote(src, group(chunk, 2 - h), z_send.at[chunk, 2], win_recv.at[chunk, 2 - h], up),
            remote(src, group(chunk, 6 - h), z_send.at[chunk, 3], win_recv.at[chunk, 6 - h], down),
        )

    def planes(chunk):
        return (
            remote(group(chunk, 4), group(chunk, 2), z_send.at[chunk, 0], win_recv.at[chunk, 2], up),
            remote(group(chunk, 3), group(chunk, 5), z_send.at[chunk, 1], win_recv.at[chunk, 5], down),
            remote(group(chunk, 3), group(chunk, 1), z_send.at[chunk, 2], win_recv.at[chunk, 1], up),
            remote(group(chunk, 4), group(chunk, 6), z_send.at[chunk, 3], win_recv.at[chunk, 6], down),
        )

    def relay(chunk):
        return (
            remote(group(chunk, 2), group(chunk, 0), z_send.at[chunk, 4], win_recv.at[chunk, 0], up),
            remote(group(chunk, 5), group(chunk, 7), z_send.at[chunk, 5], win_recv.at[chunk, 7], down),
        )

    def each(copies, act, conditions):
        for copy, there in zip(copies, conditions):

            @pl.when(there)
            def _():
                act(copy)

    def start(copies, conditions=None):
        each(copies, lambda copy: copy.start(), conditions or (above, below))

    def wait_groups(chunk, groups):
        there = (two_below, below, below, True, True, above, above, two_above)
        for g in groups:
            if there[g] is True:
                wait_group(chunk, g)
            else:
                pl.when(there[g])(functools.partial(wait_group, chunk, g))

    def inv_part(slot, to):
        if slot == 0:
            return inv_ref.at[to // 2, 1 - lax.rem(to, 2)]
        return inv_ref.at[2, lax.rem(to, 2)]

    def inv_copy(slot, d):
        to = lax.rem(y + d, 4)
        return remote(inv_part(slot, to), invs.at[slot, y], inv_send.at[slot, d - 1], inv_recv.at[slot, y], {"ph": to})

    def meta_copies(d):
        me = 4 * h + y
        to = group_member(d)
        return (
            remote(offs_ref, offs_v.at[me], meta_send.at[0, d], meta_recv.at[0, me], to),
            remote(coup_ref, coup_v.at[me], meta_send.at[1, d], meta_recv.at[1, me], to),
        )

    exchange(0).start()
    start(own(0))
    me = 4 * h + y
    pltpu.make_async_copy(offs_ref, offs_v.at[me], meta_recv.at[0, me]).start()
    pltpu.make_async_copy(coup_ref, coup_v.at[me], meta_recv.at[1, me]).start()
    for d in range(1, 8):
        for copy in meta_copies(d):
            copy.start()
    start(own(1))
    for chunk in range(1, CHUNKS):
        exchange(chunk).start()
    for slot in range(2):
        pltpu.make_async_copy(inv_part(slot, y), invs.at[slot, y], inv_recv.at[slot, y]).start()
        for d in range(1, 4):
            inv_copy(slot, d).start()
    for chunk in range(CHUNKS):
        own_local(chunk).start()

    def forward(chunk):
        if chunk < 2:
            wait_group(chunk, 4 - h)
            start(passed(chunk))
        else:
            wait_group(chunk, 3)
            wait_group(chunk, 4)
            start(planes(chunk), (above, below, above, below))

    def relays(chunk):
        wait_groups(chunk, (2, 5))
        start(relay(chunk), passes)

    def gather_meta():
        for m in range(8):
            pltpu.make_async_copy(offs_v.at[m], offs_v.at[m], meta_recv.at[0, m]).wait()
            pltpu.make_async_copy(coup_v.at[m], coup_v.at[m], meta_recv.at[1, m]).wait()
        first = pltpu.make_async_copy(offs_v, offs_s, smem_sem.at[0])
        second = pltpu.make_async_copy(coup_v, coup_s, smem_sem.at[1])
        first.start()
        second.start()
        first.wait()
        second.wait()

    def sigma_copy(chunk, n):
        to = {"en": base + n // 3, "ph": owner(chunk, n % 3)}
        part = 2 * y + h
        return remote(
            sig.at[chunk, n], whole.at[chunk, part], sig_send.at[chunk, n], sig_recv.at[chunk, part], to
        )

    def is_own(chunk, n):
        return jnp.logical_and(h == n // 3, y == owner(chunk, n % 3))

    def mix(chunk):
        wait_groups(chunk, (1, 6, 0, 7))
        if chunk < 2:
            wait_group(chunk, 3 + h)
        window = wins[chunk]

        def body(i, step, _):
            rows = pl.ds(pl.multiple_of(32 * step, 32), 32)
            total = jnp.zeros((32, window.shape[2]), jnp.float32)
            for k in range(8):
                m = 4 * (i // 3) + k // 2
                offset = offs_s[m, k % 2, i % 3]
                energy = 3 * base + i + offset
                inside = jnp.logical_and(energy >= 0, energy < 3 * n_en)
                weight = jnp.where(inside, coup_s[m, k % 2, i % 3], jnp.float32(0.0))
                slot = jnp.where(inside, i + offset + MAXOFF, MAXOFF)
                total = total + weight * window[slot, rows, :].astype(jnp.float32)
            sig[chunk, i, rows, :] = total.astype(jnp.bfloat16)
            return 0

        part = 2 * y + h

        def send(n):
            mine = is_own(chunk, n)

            @pl.when(mine)
            def _():
                pltpu.make_async_copy(sig.at[chunk, n], whole.at[chunk, part], sig_recv.at[chunk, part]).start()

            @pl.when(jnp.logical_not(mine))
            def _():
                sigma_copy(chunk, n).start()

        for n in range(6):
            lax.fori_loop(0, 2, functools.partial(body, n), 0)
            if n:
                send(n - 1)
        send(5)

    def out_ref(chunk, j):
        return (less_out, great_out)[chunk // 2].at[j, chunk % 2]

    def energy_of(chunk):
        return jnp.where(y == (chunk + 2) % 4, 2, y // 2)

    def out_copy(chunk, d):
        to = lax.rem(y + d, 4)
        j = energy_of(chunk)
        return remote(prod.at[chunk, to], out_ref(chunk, j), out_send.at[chunk, d], out_recv.at[chunk, j], {"ph": to})

    def multiply(chunk):
        @pl.when(y != chunk)
        def _():
            slot = jnp.where(y == (chunk + 2) % 4, 1, 0)
            for part in range(8):
                pltpu.make_async_copy(
                    whole.at[chunk, part], whole.at[chunk, part], sig_recv.at[chunk, part]
                ).wait()
            sigma = whole[chunk].reshape(512, 512)
            inverse = invs[slot].reshape(512, 512)

            for r in range(2):
                rows = invs[slot, pl.ds(2 * r, 2)].reshape(256, 512)
                left = jnp.dot(rows, sigma, preferred_element_type=jnp.float32).astype(jnp.bfloat16)
                result = lax.dot_general(
                    left, inverse, (((1,), (1,)), ((), ())), preferred_element_type=jnp.float32
                )
                prod[chunk, pl.ds(2 * r, 2)] = result.astype(jnp.bfloat16).reshape(2, 128, 512)
            for d in (2, 1, 3):
                out_copy(chunk, d).start()
            j = energy_of(chunk)
            pltpu.make_async_copy(prod.at[chunk, y], out_ref(chunk, j), out_recv.at[chunk, j]).start()

    def gather_inverses():
        for slot in range(2):
            for part in range(4):
                pltpu.make_async_copy(invs.at[slot, part], invs.at[slot, part], inv_recv.at[slot, part]).wait()

    forward(0)
    gather_meta()
    forward(1)
    relays(0)
    relays(1)
    forward(2)
    mix(0)
    mix(1)
    relays(2)
    forward(3)
    gather_inverses()
    multiply(0)
    mix(2)
    multiply(1)
    relays(3)
    multiply(2)
    mix(3)
    multiply(3)

    for chunk in range(CHUNKS):
        exchange(chunk).wait_send()
        sent = (own(chunk) + passed(chunk) if chunk < 2 else planes(chunk)) + relay(chunk)
        each(sent, lambda copy: copy.wait_send(), (above, below, above, below) + passes)
        for n in range(6):

            @pl.when(jnp.logical_not(is_own(chunk, n)))
            def _():
                sigma_copy(chunk, n).wait_send()

        @pl.when(y != chunk)
        def _():
            for d in range(1, 4):
                out_copy(chunk, d).wait_send()

    for slot in range(2):
        for d in range(1, 4):
            inv_copy(slot, d).wait_send()
    for d in range(1, 8):
        for copy in meta_copies(d):
            copy.wait_send()
    for chunk in range(CHUNKS):
        for j in range(3):
            pltpu.make_async_copy(out_ref(chunk, j), out_ref(chunk, j), out_recv.at[chunk, j]).wait()


def on_device(n_en, lesser_in, greater_in, inverse, offsets, couplings):
    bf16 = jnp.bfloat16
    dma = pltpu.SemaphoreType.DMA
    any_space = pl.BlockSpec(memory_space=pl.ANY)
    vmem = pl.BlockSpec(memory_space=pltpu.VMEM)
    width = lesser_in.shape[-1]
    window = pltpu.VMEM((24, ROWS, width), bf16)
    return pl.pallas_call(
        functools.partial(kernel, n_en),
        out_shape=(
            jax.ShapeDtypeStruct(lesser_in.shape, bf16),
            jax.ShapeDtypeStruct(greater_in.shape, bf16),
        ),
        in_specs=[vmem, vmem, any_space, any_space, any_space],
        out_specs=(any_space, any_space),
        scratch_shapes=[
            window, window, window, window,
            pltpu.VMEM((CHUNKS, 6, ROWS, width), bf16),
            pltpu.VMEM((CHUNKS, 8, ROWS, width), bf16),
            pltpu.VMEM((2, 4, 128, width), bf16),
            pltpu.VMEM((CHUNKS, 4, 128, width), bf16),
            pltpu.VMEM((8, 2, 3), jnp.int32),
            pltpu.VMEM((8, 2, 3), jnp.float32),
            pltpu.SMEM((8, 2, 3), jnp.int32),
            pltpu.SMEM((8, 2, 3), jnp.float32),
            dma((CHUNKS, 8)),
            dma((CHUNKS,)),
            dma((CHUNKS, 6)),
            dma((CHUNKS, 6)),
            dma((CHUNKS, 8)),
            dma((2, 3)),
            dma((2, 4)),
            dma((CHUNKS, 4)),
            dma((CHUNKS, 3)),
            dma((2, 8)),
            dma((2, 8)),
            dma((2,)),
        ],
        compiler_params=pltpu.CompilerParams(collective_id=0, has_side_effects=True, vmem_limit_bytes=40 * 1024 * 1024),
        name="born_update",
    )(offsets.T, couplings.T, *(pltpu.with_memory_space_constraint(a, pltpu.HBM) for a in (lesser_in, greater_in, inverse)))


def solution(mesh):
    blocks = P("en", "blk", "ph", None)
    placed = (blocks, blocks, blocks, P("en", "ph"), P("en", "ph"))
    return jax.shard_map(
        functools.partial(on_device, mesh.shape["en"]),
        mesh=mesh,
        in_specs=placed,
        out_specs=(blocks, blocks),
        check_vma=False,
    )
```

```python
import functools

import jax
import jax.numpy as jnp
from jax import lax
from jax.experimental import pallas as pl
from jax.experimental.pallas import tpu as pltpu
from jax.sharding import PartitionSpec as P

MESH = pl.DeviceIdType.MESH
MAXOFF = 9
CHUNKS = 4
EXTRA = 3
ROWS = 64


def owner(chunk, j):
    if j == 2:
        return (chunk + 2) % 4
    return 2 * j + 1 - chunk % 2


def kernel(
    n_en, offs_ref, coup_ref, less_ref, great_ref, inv_ref,
    less_out, great_out,
    win0, win1, win2, win3, sig, whole, invs, prod, offs_v, coup_v, offs_s, coup_s,
    win_recv, x_send, z_send, sig_send, sig_recv, inv_send, inv_recv,
    out_send, out_recv, meta_send, meta_recv, smem_sem,
):
    wins = (win0, win1, win2, win3)
    en, y = lax.axis_index("en"), lax.axis_index("ph")
    h = lax.rem(en, 2)
    base = en - h
    above, below = en + 2 < n_en, en >= 2
    two_above, two_below = en + 4 < n_en, en >= 4
    up = {"en": lax.rem(en + 2, n_en)}
    down = {"en": lax.rem(en + n_en - 2, n_en)}
    partner = {"en": base + 1 - h}

    def group_member(d):
        return {"en": base + lax.rem(h + d // 4, 2), "ph": lax.rem(y + d % 4, 4)}

    barrier = pltpu.get_barrier_semaphore()
    for side, there in ((up, above), (down, below)):

        @pl.when(there)
        def _():
            pl.semaphore_signal(barrier, inc=1, device_id=side, device_id_type=MESH)

    for d in range(1, 8):
        pl.semaphore_signal(barrier, inc=1, device_id=group_member(d), device_id_type=MESH)
    pl.semaphore_wait(barrier, 7 + above.astype(jnp.int32) + below.astype(jnp.int32))

    def remote(src, dst, send, recv, device):
        return pltpu.make_async_remote_copy(
            src_ref=src, dst_ref=dst, send_sem=send, recv_sem=recv, device_id=device, device_id_type=MESH
        )

    passes = (jnp.logical_and(above, below),) * 2

    def source(chunk, half):
        ref = (less_ref, great_ref)[chunk // 2]
        return ref.at[:, chunk % 2, pl.ds(pl.multiple_of(half * ROWS, ROWS), ROWS), :]

    def group(chunk, g):
        return wins[chunk].at[pl.ds(3 * g, 3)]

    def wait_group(chunk, g):
        pltpu.make_async_copy(group(chunk, g), group(chunk, g), win_recv.at[chunk, g]).wait()

    def own_local(chunk):
        return pltpu.make_async_copy(source(chunk, h), group(chunk, 3 + h), win_recv.at[chunk, 3 + h])

    def exchange(chunk):
        return remote(source(chunk, 1 - h), group(chunk, 3 + h), x_send.at[chunk], win_recv.at[chunk, 3 + h], partner)

    def own(chunk):
        src = source(chunk, h)
        return (
            remote(src, group(chunk, 1 + h), z_send.at[chunk, 0], win_recv.at[chunk, 1 + h], up),
            remote(src, group(chunk, 5 + h), z_send.at[chunk, 1], win_recv.at[chunk, 5 + h], down),
        )

    def passed(chunk):
        src = group(chunk, 4 - h)
        return (
            remote(src, group(chunk, 2 - h), z_send.at[chunk, 2], win_recv.at[chunk, 2 - h], up),
            remote(src, group(chunk, 6 - h), z_send.at[chunk, 3], win_recv.at[chunk, 6 - h], down),
        )

    def planes(chunk):
        return (
            remote(group(chunk, 4), group(chunk, 2), z_send.at[chunk, 0], win_recv.at[chunk, 2], up),
            remote(group(chunk, 3), group(chunk, 5), z_send.at[chunk, 1], win_recv.at[chunk, 5], down),
            remote(group(chunk, 3), group(chunk, 1), z_send.at[chunk, 2], win_recv.at[chunk, 1], up),
            remote(group(chunk, 4), group(chunk, 6), z_send.at[chunk, 3], win_recv.at[chunk, 6], down),
        )

    def relay(chunk):
        return (
            remote(group(chunk, 2), group(chunk, 0), z_send.at[chunk, 4], win_recv.at[chunk, 0], up),
            remote(group(chunk, 5), group(chunk, 7), z_send.at[chunk, 5], win_recv.at[chunk, 7], down),
        )

    def each(copies, act, conditions):
        for copy, there in zip(copies, conditions):

            @pl.when(there)
            def _():
                act(copy)

    def start(copies, conditions=None):
        each(copies, lambda copy: copy.start(), conditions or (above, below))

    def wait_groups(chunk, groups):
        there = (two_below, below, below, True, True, above, above, two_above)
        for g in groups:
            if there[g] is True:
                wait_group(chunk, g)
            else:
                pl.when(there[g])(functools.partial(wait_group, chunk, g))

    def inv_part(slot, to):
        if slot == 0:
            return inv_ref.at[to // 2, 1 - lax.rem(to, 2)]
        return inv_ref.at[2, lax.rem(to, 2)]

    def inv_copy(slot, d):
        to = lax.rem(y + d, 4)
        return remote(inv_part(slot, to), invs.at[slot, y], inv_send.at[slot, d - 1], inv_recv.at[slot, y], {"ph": to})

    def meta_copies(d):
        me = 4 * h + y
        to = group_member(d)
        return (
            remote(offs_ref, offs_v.at[me], meta_send.at[0, d], meta_recv.at[0, me], to),
            remote(coup_ref, coup_v.at[me], meta_send.at[1, d], meta_recv.at[1, me], to),
        )

    exchange(0).start()
    start(own(0))
    me = 4 * h + y
    pltpu.make_async_copy(offs_ref, offs_v.at[me], meta_recv.at[0, me]).start()
    pltpu.make_async_copy(coup_ref, coup_v.at[me], meta_recv.at[1, me]).start()
    for d in range(1, 8):
        for copy in meta_copies(d):
            copy.start()
    start(own(1))
    for chunk in range(1, CHUNKS):
        exchange(chunk).start()
    for slot in range(2):
        pltpu.make_async_copy(inv_part(slot, y), invs.at[slot, y], inv_recv.at[slot, y]).start()
        for d in range(1, 4):
            inv_copy(slot, d).start()
    for chunk in range(CHUNKS):
        own_local(chunk).start()

    def forward(chunk):
        if chunk < 2:
            wait_group(chunk, 4 - h)
            start(passed(chunk))
        else:
            wait_group(chunk, 3)
            wait_group(chunk, 4)
            start(planes(chunk), (above, below, above, below))

    def relays(chunk):
        wait_groups(chunk, (2, 5))
        start(relay(chunk), passes)

    def gather_meta():
        for m in range(8):
            pltpu.make_async_copy(offs_v.at[m], offs_v.at[m], meta_recv.at[0, m]).wait()
            pltpu.make_async_copy(coup_v.at[m], coup_v.at[m], meta_recv.at[1, m]).wait()
        first = pltpu.make_async_copy(offs_v, offs_s, smem_sem.at[0])
        second = pltpu.make_async_copy(coup_v, coup_s, smem_sem.at[1])
        first.start()
        second.start()
        first.wait()
        second.wait()

    def sigma_copy(chunk, n):
        to = {"en": base + n // 3, "ph": owner(chunk, n % 3)}
        part = 2 * y + h
        return remote(
            sig.at[chunk, n], whole.at[chunk, part], sig_send.at[chunk, n], sig_recv.at[chunk, part], to
        )

    def is_own(chunk, n):
        return jnp.logical_and(h == n // 3, y == owner(chunk, n % 3))

    def mix(chunk):
        wait_groups(chunk, (1, 6, 0, 7))
        if chunk < 2:
            wait_group(chunk, 3 + h)
        window = wins[chunk]

        def body(i, step, _):
            rows = pl.ds(pl.multiple_of(32 * step, 32), 32)
            total = jnp.zeros((32, window.shape[2]), jnp.float32)
            for k in range(8):
                m = 4 * (i // 3) + k // 2
                offset = offs_s[m, k % 2, i % 3]
                energy = 3 * base + i + offset
                inside = jnp.logical_and(energy >= 0, energy < 3 * n_en)
                weight = jnp.where(inside, coup_s[m, k % 2, i % 3], jnp.float32(0.0))
                slot = jnp.where(inside, i + offset + MAXOFF, MAXOFF)
                total = total + weight * window[slot, rows, :].astype(jnp.float32)
            sig[chunk, i, rows, :] = total.astype(jnp.bfloat16)
            return 0

        part = 2 * y + h

        def send(n):
            mine = is_own(chunk, n)

            @pl.when(mine)
            def _():
                pltpu.make_async_copy(sig.at[chunk, n], whole.at[chunk, part], sig_recv.at[chunk, part]).start()

            @pl.when(jnp.logical_not(mine))
            def _():
                sigma_copy(chunk, n).start()

        for n in range(6):
            lax.fori_loop(0, 2, functools.partial(body, n), 0)
            if n:
                send(n - 1)
        send(5)

    def out_ref(chunk, j):
        return (less_out, great_out)[chunk // 2].at[j, chunk % 2]

    def energy_of(chunk):
        return jnp.where(y == (chunk + 2) % 4, 2, y // 2)

    def out_copy(chunk, d):
        to = lax.rem(y + d, 4)
        j = energy_of(chunk)
        return remote(prod.at[chunk, to], out_ref(chunk, j), out_send.at[chunk, d], out_recv.at[chunk, j], {"ph": to})

    def multiply(chunk):
        @pl.when(y != chunk)
        def _():
            slot = jnp.where(y == (chunk + 2) % 4, 1, 0)
            for part in range(8):
                pltpu.make_async_copy(
                    whole.at[chunk, part], whole.at[chunk, part], sig_recv.at[chunk, part]
                ).wait()
            sigma = whole[chunk].reshape(512, 512)
            inverse = invs[slot].reshape(512, 512)

            for r in (1 - y // 2, y // 2):
                rows = invs[slot, pl.ds(2 * r, 2)].reshape(256, 512)
                left = jnp.dot(rows, sigma, preferred_element_type=jnp.float32).astype(jnp.bfloat16)
                result = lax.dot_general(
                    left, inverse, (((1,), (1,)), ((), ())), preferred_element_type=jnp.float32
                )
                prod[chunk, pl.ds(2 * r, 2)] = result.astype(jnp.bfloat16).reshape(2, 128, 512)
                for d in (2, 1, 3, 0):

                    @pl.when(lax.rem(y + d, 4) // 2 == r)
                    def _():
                        if d:
                            out_copy(chunk, d).start()
                        else:
                            j = energy_of(chunk)
                            pltpu.make_async_copy(prod.at[chunk, y], out_ref(chunk, j), out_recv.at[chunk, j]).start()

    def gather_inverses():
        for slot in range(2):
            for part in range(4):
                pltpu.make_async_copy(invs.at[slot, part], invs.at[slot, part], inv_recv.at[slot, part]).wait()

    forward(0)
    gather_meta()
    forward(1)
    relays(0)
    relays(1)
    forward(2)
    mix(0)
    mix(1)
    relays(2)
    forward(3)
    gather_inverses()
    multiply(0)
    mix(2)
    multiply(1)
    relays(3)
    multiply(2)
    mix(3)
    multiply(3)

    for chunk in range(CHUNKS):
        exchange(chunk).wait_send()
        sent = (own(chunk) + passed(chunk) if chunk < 2 else planes(chunk)) + relay(chunk)
        each(sent, lambda copy: copy.wait_send(), (above, below, above, below) + passes)
        for n in range(6):

            @pl.when(jnp.logical_not(is_own(chunk, n)))
            def _():
                sigma_copy(chunk, n).wait_send()

        @pl.when(y != chunk)
        def _():
            for d in range(1, 4):
                out_copy(chunk, d).wait_send()

    for slot in range(2):
        for d in range(1, 4):
            inv_copy(slot, d).wait_send()
    for d in range(1, 8):
        for copy in meta_copies(d):
            copy.wait_send()
    for chunk in range(CHUNKS):
        for j in range(3):
            pltpu.make_async_copy(out_ref(chunk, j), out_ref(chunk, j), out_recv.at[chunk, j]).wait()


def on_device(n_en, lesser_in, greater_in, inverse, offsets, couplings):
    bf16 = jnp.bfloat16
    dma = pltpu.SemaphoreType.DMA
    any_space = pl.BlockSpec(memory_space=pl.ANY)
    vmem = pl.BlockSpec(memory_space=pltpu.VMEM)
    width = lesser_in.shape[-1]
    window = pltpu.VMEM((24, ROWS, width), bf16)
    return pl.pallas_call(
        functools.partial(kernel, n_en),
        out_shape=(
            jax.ShapeDtypeStruct(lesser_in.shape, bf16),
            jax.ShapeDtypeStruct(greater_in.shape, bf16),
        ),
        in_specs=[vmem, vmem, any_space, any_space, any_space],
        out_specs=(any_space, any_space),
        scratch_shapes=[
            window, window, window, window,
            pltpu.VMEM((CHUNKS, 6, ROWS, width), bf16),
            pltpu.VMEM((CHUNKS, 8, ROWS, width), bf16),
            pltpu.VMEM((2, 4, 128, width), bf16),
            pltpu.VMEM((CHUNKS, 4, 128, width), bf16),
            pltpu.VMEM((8, 2, 3), jnp.int32),
            pltpu.VMEM((8, 2, 3), jnp.float32),
            pltpu.SMEM((8, 2, 3), jnp.int32),
            pltpu.SMEM((8, 2, 3), jnp.float32),
            dma((CHUNKS, 8)),
            dma((CHUNKS,)),
            dma((CHUNKS, 6)),
            dma((CHUNKS, 6)),
            dma((CHUNKS, 8)),
            dma((2, 3)),
            dma((2, 4)),
            dma((CHUNKS, 4)),
            dma((CHUNKS, 3)),
            dma((2, 8)),
            dma((2, 8)),
            dma((2,)),
        ],
        compiler_params=pltpu.CompilerParams(collective_id=0, has_side_effects=True, vmem_limit_bytes=40 * 1024 * 1024),
        name="born_update",
    )(offsets.T, couplings.T, *(pltpu.with_memory_space_constraint(a, pltpu.HBM) for a in (lesser_in, greater_in, inverse)))


def solution(mesh):
    blocks = P("en", "blk", "ph", None)
    placed = (blocks, blocks, blocks, P("en", "ph"), P("en", "ph"))
    return jax.shard_map(
        functools.partial(on_device, mesh.shape["en"]),
        mesh=mesh,
        in_specs=placed,
        out_specs=(blocks, blocks),
        check_vma=False,
    )
```
